32 devices in a mesh: row: 8 (over z, y), col: 4 (over x, core).
Axes of the slice: x: 2, y: 2, z: 4, core: 2. Of those that a mesh axis runs over, the one named last changes fastest.
Arguments:
- tokens: bfloat16 [8192, 1472], P(('row', 'col')), may hold values from -6 to 6
- lengths: int32 [8], P('row'), may hold values from 200 to 1024, as said below
- out_grad: bfloat16 [8192, 1472], P(('row', 'col')), may hold values from -6 to 6
- gain_attn: float32 [1472], replicated, may hold values from 0.5 to 1.5
- w_query: bfloat16 [1472, 384], P('row', 'col'), may hold values from -0.0390625 to 0.0390625
- w_key: bfloat16 [1472, 384], P('row', 'col'), may hold values from -0.15625 to 0.15625
- w_value: bfloat16 [1472, 384], P('row', 'col'), may hold values from -0.15625 to 0.15625
- w_attn_out: bfloat16 [384, 1472], P('col', 'row'), may hold values from -1.25 to 1.25
- bias_table: float32 [32, 6], replicated, may hold values from -4 to 4
- gain_ff: float32 [1472], replicated, may hold values from 0.5 to 1.5
- w_gate: bfloat16 [1472, 3584], P('row', 'col'), may hold values from -0.15625 to 0.15625
- w_up: bfloat16 [1472, 3584], P('row', 'col'), may hold values from -0.15625 to 0.15625
- w_down: bfloat16 [3584, 1472], P('col', 'row'), may hold values from -0.09375 to 0.09375
Outputs:
- output: bfloat16 [8192, 1472], P(('row', 'col'))
- input_grad: float32 [8192, 1472], P(('row', 'col'))
- grad_gain_attn: float32 [1472], replicated
- grad_query: float32 [1472, 384], P('row', 'col')
- grad_key: float32 [1472, 384], P('row', 'col')
- grad_value: float32 [1472, 384], P('row', 'col')
- grad_attn_out: float32 [384, 1472], P('col', 'row')
- grad_bias: float32 [32, 6], replicated
- grad_gain_ff: float32 [1472], replicated
- grad_gate: float32 [1472, 3584], P('row', 'col')
- grad_up: float32 [1472, 3584], P('row', 'col')
- grad_down: float32 [3584, 1472], P('col', 'row')
The draws below stay inside these ranges and needn't reach their ends.
Inputs may be any that keep to these rules, and one draw needn't show every extreme that they name: Each sequence holds one document in its first lengths slots, the rest of its 1024 slots are padding; some sequence is full.
All inputs are finite; a program needn't handle non-finite values.
Results may differ from the reference program's by a relative error of at most 0.023.
Values may be sent and summed in bfloat16 or wider, within the bound.
No kernel may reach another device: no remote copies, remote signals or barrier semaphores. Data moves between devices by JAX's collectives and lax.ppermute only.
A program may use at most 192 MiB of HBM per device.

```python
from functools import partial
import jax
import jax.numpy as jnp
from jax import lax

D = 1472
FF = 3584
HEADS = 6
HEAD_DIM = 64
BUCKETS = 32
LEN_MIN = 200
SEQ = 1024
SEQS = 8
TOKENS = 8192


def draw_lengths(key, part):
    key_draw, key_pick = jax.random.split(key)
    lengths_drawn = jax.random.randint(key_draw, (SEQS,), LEN_MIN, SEQ + 1)
    longest_index = jax.random.randint(key_pick, (), 0, SEQS)
    return jnp.where(jnp.arange(SEQS) == longest_index, SEQ, lengths_drawn).astype(jnp.int32)


def block_levels(stream_key, extent, cuts, least, top_value):
    def one(axis_at, blocks):
        heights = jax.random.uniform(jax.random.fold_in(jax.random.fold_in(stream_key, 6), axis_at), (blocks,), jnp.float32, least / len(cuts), top_value / len(cuts))
        return jnp.repeat(jnp.exp(heights), extent[axis_at] // blocks).reshape((-1,) + (1,) * (len(extent) - axis_at - 1))

    level = one(*cuts[0])
    for cut in cuts[1:]:
        level = level * one(*cut)
    return level


def gaussian(stream_key, dims, width, reach, pieces=(), kind=jnp.bfloat16):
    values = width * jax.random.normal(stream_key, dims, jnp.float32)
    if pieces:
        values = values * block_levels(stream_key, dims, pieces, -0.22, 0.18)
    return jnp.clip(values, -reach, reach).astype(kind)


def setup_inputs(seed: int = 0) -> dict:
    key_list = jax.random.split(jax.random.key(seed), 14)
    return {
        "tokens": gaussian(key_list[0], (TOKENS, D), 1.0, 6.0, ((0, 32),)),
        "lengths": draw_lengths(jax.random.fold_in(key_list[13], 71), 0),
        "out_grad": gaussian(key_list[2], (TOKENS, D), 1.0, 6.0, ((0, 32),)),
        "gain_attn": jnp.clip(1.0 + 0.1 * jax.random.normal(key_list[3], (D,), jnp.float32), 0.5, 1.5),
        "w_query": gaussian(key_list[4], (D, HEADS * HEAD_DIM), (16 * D) ** -0.5, 0.0390625, ((0, 8), (1, 4))),
        "w_key": gaussian(key_list[5], (D, HEADS * HEAD_DIM), D ** -0.5, 0.15625, ((0, 8), (1, 4))),
        "w_value": gaussian(key_list[6], (D, HEADS * HEAD_DIM), D ** -0.5, 0.15625, ((0, 8), (1, 4))),
        "w_attn_out": gaussian(key_list[7], (HEADS * HEAD_DIM, D), (HEADS * HEAD_DIM // 16) ** -0.5, 1.25, ((0, 4), (1, 8))),
        "bias_table": gaussian(key_list[8], (BUCKETS, HEADS), 1.0, 4.0, (), jnp.float32),
        "gain_ff": jnp.clip(1.0 + 0.1 * jax.random.normal(key_list[9], (D,), jnp.float32), 0.5, 1.5),
        "w_gate": gaussian(key_list[10], (D, FF), D ** -0.5, 0.15625, ((0, 8), (1, 4))),
        "w_up": gaussian(key_list[11], (D, FF), D ** -0.5, 0.15625, ((0, 8), (1, 4))),
        "w_down": gaussian(key_list[12], (FF, D), FF ** -0.5, 0.09375, ((0, 4), (1, 8))),
    }


@jax.custom_vjp
def low(v):
    return lax.optimization_barrier(v.astype(jnp.bfloat16)).astype(jnp.float32)

@jax.custom_vjp
def low_back(v):
    return v

def low_keep(v):
    return (low(v), None)

def low_pass(kept, grad):
    return (grad,)

def back_keep(v):
    return (v, None)

def back_low(kept, grad):
    return (low(grad),)
low.defvjp(low_keep, low_pass)
low_back.defvjp(back_keep, back_low)
EPSILON = 1e-06
FAR_STEPS = (12, 16, 23, 32, 46, 64, 91)
PRECISION_MAX = lax.Precision.HIGHEST

def bucket_index(offsets):
    magnitude = jnp.abs(offsets)
    far_bucket = 8 + sum(((magnitude >= limit).astype(jnp.int32) for limit in FAR_STEPS))
    near_bucket = jnp.where(magnitude < 8, magnitude, far_bucket)
    return (near_bucket + jnp.where(offsets > 0, 16, 0)).astype(jnp.int32)

def root_scale(values, gain):
    return values * lax.rsqrt(lax.optimization_barrier(jnp.mean(values * values, axis=-1, keepdims=True)) + EPSILON) * gain

def matmul(left, right):
    return jnp.dot(left, right, precision=PRECISION_MAX, preferred_element_type=jnp.float32)

def attend_head(packed, length):
    query_head, key_head, value_head, table_line = packed
    positions = jnp.arange(SEQ, dtype=jnp.int32)
    buckets = bucket_index(positions[None, :] - positions[:, None])
    onehot = (buckets[:, :, None] == jnp.arange(BUCKETS, dtype=jnp.int32)[None, None, :]).astype(jnp.float32)
    bias_full = lax.optimization_barrier(jnp.sum(onehot * table_line[None, None, :], axis=-1))
    scores = jnp.dot(query_head, key_head.T, precision=PRECISION_MAX, preferred_element_type=jnp.float32) + bias_full
    scores = low_back(scores)
    masked = jnp.where((positions < length)[None, :], scores, -1e+30)
    attention = low(jax.nn.softmax(masked, axis=-1))
    return jnp.dot(attention, value_head, precision=PRECISION_MAX, preferred_element_type=jnp.float32)

def attend_sequence(packed, bias_table):
    queries, keys, values, length = packed
    split_query = jnp.transpose(queries.reshape(SEQ, HEADS, HEAD_DIM), (1, 0, 2))
    split_key = jnp.transpose(keys.reshape(SEQ, HEADS, HEAD_DIM), (1, 0, 2))
    split_value = jnp.transpose(values.reshape(SEQ, HEADS, HEAD_DIM), (1, 0, 2))
    mixed = lax.map(jax.checkpoint(partial(attend_head, length=length)), (split_query, split_key, split_value, bias_table.T))
    return jnp.transpose(mixed, (1, 0, 2)).reshape(SEQ, HEADS * HEAD_DIM)

def reference(tokens, lengths, out_grad, gain_attn, w_query, w_key, w_value, w_attn_out, bias_table, gain_ff, w_gate, w_up, w_down):
    positions = jnp.arange(TOKENS, dtype=jnp.int32) % SEQ
    sequence_ids = jnp.arange(TOKENS, dtype=jnp.int32) // SEQ
    row_mask = (positions < lengths[sequence_ids]).astype(jnp.float32)[:, None]
    inner_width = HEADS * HEAD_DIM

    def forward(inputs, gain_one, query_w, key_w, value_w, out_w, table, gain_two, gate_w, up_w, down_w):
        normed = low(root_scale(inputs, gain_one))
        queries = low_back(low(matmul(normed, query_w)))
        keys = low_back(low(matmul(normed, key_w)))
        values = low_back(low(matmul(normed, value_w)))
        mixed = lax.map(jax.checkpoint(partial(attend_sequence, bias_table=table)), (queries.reshape(SEQS, SEQ, inner_width), keys.reshape(SEQS, SEQ, inner_width), values.reshape(SEQS, SEQ, inner_width), lengths))
        context = low_back(low(mixed.reshape(TOKENS, inner_width)))
        hidden = inputs + low_back(matmul(context, out_w))
        normed_ff = low(root_scale(hidden, gain_two))
        gate_proj = low_back(matmul(normed_ff, gate_w))
        up_proj = low_back(matmul(normed_ff, up_w))
        hidden_ff = low(jax.nn.gelu(gate_proj, approximate=True) * up_proj)
        ff_branch = low_back(matmul(hidden_ff, down_w))
        return row_mask * (hidden + ff_branch)
    floats = tuple((item.astype(jnp.float32) for item in (tokens, gain_attn, w_query, w_key, w_value, w_attn_out, bias_table, gain_ff, w_gate, w_up, w_down)))
    result, pullback = jax.vjp(forward, *floats)
    gradients = pullback(out_grad.astype(jnp.float32))
    return (result.astype(jnp.bfloat16), gradients[0], gradients[1], gradients[2], gradients[3], gradients[4], gradients[5], gradients[6], gradients[7], gradients[8], gradients[9], gradients[10])
```

```python
from functools import partial

import jax
import jax.numpy as jnp
from jax import lax
from jax.experimental import pallas as pl
from jax.experimental.pallas import tpu as pltpu
from jax.sharding import PartitionSpec as P

HEADS = 6
HEAD_DIM = 64


EPSILON = 1e-06
FAR_STEPS = (12, 16, 23, 32, 46, 64, 91)
PRECISION_MAX = lax.Precision.HIGHEST
F32 = jnp.float32
BF16 = jnp.bfloat16
LANES = 128
MASKED = -1e30
GELU_SCALE = 0.7978845608028654
GELU_CUBE = 0.044715

NN = (((1,), (0,)), ((), ()))
NT = (((1,), (1,)), ((), ()))
TN = (((0,), (0,)), ((), ()))


def dot(left, right, dims=NN):
    return lax.dot_general(left, right, dims, preferred_element_type=F32)


def whole(memory=None):
    if memory is None:
        return pl.BlockSpec(pipeline_mode=pl.Buffered(1))
    return pl.BlockSpec(memory_space=memory)


def fixed(shape):
    zeros = (0,) * len(shape)
    return pl.BlockSpec(shape, lambda *_: zeros, pipeline_mode=pl.Buffered(1))


def wide(column, width):
    return jnp.concatenate([column] * (width // LANES), axis=1)


def params(mib):
    return pltpu.CompilerParams(vmem_limit_bytes=mib * 1024 * 1024)


def cost(flops, moved, exps=0):
    return pl.CostEstimate(flops=int(flops), bytes_accessed=int(moved), transcendentals=int(exps))


def pick(own, other, core, slot):
    return jnp.where(core == slot, own, other)


def qkv_kernel(info, blocks, gain, w_own, w_other, normed_out, q_out, k_out, v_out, weight):
    step = pl.program_id(0)
    core = info[1]
    rows = w_own.shape[2]

    @pl.when(step == 0)
    def _():
        for part in range(3):
            for slot in range(2):
                block = pick(w_own[part], w_other[part], core, slot)
                weight[(2 * part + slot) * rows : (2 * part + slot + 1) * rows, :] = block.T

    values = blocks[0].astype(F32)
    scale = lax.rsqrt(jnp.mean(values * values, axis=0, keepdims=True) + EPSILON)
    normed = (values * scale * wide(gain[...], values.shape[1])).astype(BF16)
    normed_out[0] = normed
    width = 2 * rows
    k_out[...] = dot(weight[width : 2 * width, :], normed).astype(BF16)
    v_out[...] = dot(weight[2 * width :, :], normed).astype(BF16)

    @pl.when(step < 2)
    def _():
        q_out[...] = dot(weight[:width, :], normed).astype(BF16)


def qkv_call(info, blocks, gain, w_own, w_other):
    count, depth, width = blocks.shape
    rows = w_own.shape[2]
    tall = 2 * rows
    return pl.pallas_call(
        qkv_kernel,
        out_shape=(
            jax.ShapeDtypeStruct((count, depth, width), BF16),
            jax.ShapeDtypeStruct((tall, 2 * width), BF16),
            jax.ShapeDtypeStruct((tall, count * width), BF16),
            jax.ShapeDtypeStruct((tall, count * width), BF16),
        ),
        grid=(count,),
        in_specs=[
            whole(pltpu.SMEM),
            pl.BlockSpec((1, depth, width), lambda i: (i, 0, 0)),
            fixed((depth, LANES)),
            fixed(w_own.shape),
            fixed(w_other.shape),
        ],
        out_specs=(
            pl.BlockSpec((1, depth, width), lambda i: (i, 0, 0)),
            pl.BlockSpec((tall, width), lambda i: (0, jnp.minimum(i, 1))),
            pl.BlockSpec((tall, width), lambda i: (0, i)),
            pl.BlockSpec((tall, width), lambda i: (0, i)),
        ),
        scratch_shapes=[pltpu.VMEM((3 * tall, depth), BF16)],
        compiler_params=params(32),
        cost_estimate=cost(2 * depth * tall * width * 10, 14e6),
        name="qkv",
    )(info, blocks, gain, w_own, w_other)


def bucket_of(offsets):
    magnitude = jnp.abs(offsets)
    far_bucket = 8
    for limit in FAR_STEPS:
        far_bucket = far_bucket + (magnitude >= limit).astype(jnp.int32)
    near_bucket = jnp.where(magnitude < 8, magnitude, far_bucket)
    return near_bucket + jnp.where(offsets > 0, 16, 0)


def strip_offsets(start, rows):
    down = lax.broadcasted_iota(jnp.int32, (rows, LANES), 0)
    across = lax.broadcasted_iota(jnp.int32, (rows, LANES), 1)
    return down + start - across


def attend_kernel(info, table, q_ref, k_ref, v_ref, att_out, ctx_out, strip, scores):
    head, half = pl.program_id(0), pl.program_id(1)
    span = k_ref.shape[1]
    width = q_ref.shape[1]
    column = info[0] * pl.num_programs(0) + head

    @pl.when(half == 0)
    def _():
        low, high = span - LANES, span + 2 * LANES
        strip[:low, :] = jnp.full((low, LANES), table[15, column], F32)
        strip[high:, :] = jnp.full((2 * span - high, LANES), table[31, column], F32)
        for piece in range(3):
            offsets = strip_offsets((piece - 1) * LANES, LANES)
            bucket = bucket_of(offsets)
            bias = jnp.full(bucket.shape, table[0, column], F32)
            for entry in range(1, 32):
                bias = jnp.where(bucket == entry, table[entry, column], bias)
            strip[low + piece * LANES : low + (piece + 1) * LANES, :] = bias

    query = q_ref[...]
    query_base = info[3 + half]
    length = info[2]
    subs = width // LANES
    peak = jnp.full((8, width), MASKED, F32)
    for block in range(span // LANES):
        key_base = info[3 + block // subs] + (block % subs) * LANES
        tile = dot(k_ref[:, block * LANES : (block + 1) * LANES], query, TN)
        first = span + key_base - query_base
        bias = [
            strip[pl.ds(pl.multiple_of(first - LANES * sub, LANES), LANES), :] for sub in range(subs)
        ]
        tile = tile + jnp.concatenate(bias, axis=1)
        position = key_base + lax.broadcasted_iota(jnp.int32, tile.shape, 0)
        tile = jnp.where(position < length, tile, MASKED)
        scores[block * LANES : (block + 1) * LANES, :] = tile
        peak = jnp.maximum(peak, jnp.max(tile.reshape(LANES // 8, 8, width), axis=0))
    top = jnp.max(peak, axis=0, keepdims=True)
    total = jnp.zeros((8, width), F32)
    for block in range(span // LANES):
        part = pl.ds(block * LANES, LANES)
        tile = jnp.exp(scores[part, :] - top)
        scores[part, :] = tile
        total = total + jnp.sum(tile.reshape(LANES // 8, 8, width), axis=0)
    inverse = 1.0 / jnp.sum(total, axis=0, keepdims=True)
    for block in range(span // LANES):
        part = pl.ds(block * LANES, LANES)
        att_out[0, part, :] = (scores[part, :] * inverse).astype(BF16)
    ctx_out[...] = dot(v_ref[...], att_out[0]).astype(BF16)


def attend_call(info, table, queries, keys, values):
    tall, span = keys.shape
    width = queries.shape[1] // 2
    heads = tall // HEAD_DIM
    return pl.pallas_call(
        attend_kernel,
        out_shape=(
            jax.ShapeDtypeStruct((heads, span, 2 * width), BF16),
            jax.ShapeDtypeStruct((tall, 2 * width), BF16),
        ),
        grid=(heads, 2),
        in_specs=[
            whole(pltpu.SMEM),
            whole(pltpu.SMEM),
            pl.BlockSpec((HEAD_DIM, width), lambda h, i: (h, i)),
            pl.BlockSpec((HEAD_DIM, span), lambda h, i: (h, 0)),
            pl.BlockSpec((HEAD_DIM, span), lambda h, i: (h, 0)),
        ],
        out_specs=(
            pl.BlockSpec((1, span, width), lambda h, i: (h, 0, i)),
            pl.BlockSpec((HEAD_DIM, width), lambda h, i: (h, i)),
        ),
        scratch_shapes=[pltpu.VMEM((2 * span, LANES), F32), pltpu.VMEM((span, width), F32)],
        compiler_params=params(24),
        cost_estimate=cost(heads * span * width * 2 * 1024, 6e6, heads * span * width * 2),
        name="attend",
    )(info, table, queries, keys, values)


def attend_back_kernel(
    info, att_ref, g_ref, q_ref, k_ref, v_ref, dq_out, dk_out, dv_out, bias_out, strip, dots, dsc
):
    half = pl.program_id(1)
    span = k_ref.shape[1]
    width = q_ref.shape[1]
    subs = width // LANES
    grad = g_ref[...]

    @pl.when(half == 0)
    def _():
        strip[...] = jnp.zeros_like(strip)

    inner = jnp.zeros((8, width), F32)
    for block in range(span // LANES):
        part = pl.ds(block * LANES, LANES)
        tile = dot(v_ref[:, block * LANES : (block + 1) * LANES], grad, TN)
        dots[part, :] = tile
        weighted = att_ref[0, part, :].astype(F32) * tile
        inner = inner + jnp.sum(weighted.reshape(LANES // 8, 8, width), axis=0)
    inner = jnp.sum(inner, axis=0, keepdims=True)
    query_base = info[3 + half]
    for block in range(span // LANES):
        part = pl.ds(block * LANES, LANES)
        tile = (att_ref[0, part, :].astype(F32) * (dots[part, :] - inner)).astype(BF16)
        dsc[part, :] = tile
        tile = tile.astype(F32)
        key_base = info[3 + block // subs] + (block % subs) * LANES
        first = span + key_base - query_base
        for sub in range(subs):
            rows = pl.ds(pl.multiple_of(first - LANES * sub, LANES), LANES)
            strip[rows, :] = strip[rows, :] + tile[:, sub * LANES : (sub + 1) * LANES]
    dq_out[...] = dot(k_ref[...], dsc[...]).astype(BF16)
    dv = dot(grad, att_ref[0], NT)
    dk = dot(q_ref[...], dsc[...], NT)

    @pl.when(half == 0)
    def _():
        dk_out[...] = dk
        dv_out[...] = dv

    @pl.when(half == 1)
    def _():
        dk_out[...] = dk_out[...] + dk
        dv_out[...] = dv_out[...] + dv
        low, high = span - LANES, span + 2 * LANES
        fold = lambda tile: jnp.sum(tile.reshape(tile.shape[0] // 8, 8, LANES), axis=0)
        sums = [jnp.zeros((8, LANES), F32) for _ in range(32)]
        sums[15] = fold(strip[:low, :])
        sums[31] = fold(strip[high:, :])
        for piece in range(3):
            bucket = bucket_of(strip_offsets((piece - 1) * LANES, LANES))
            tile = strip[low + piece * LANES : low + (piece + 1) * LANES, :]
            entries = (range(1, 16), range(32), range(17, 32))[piece]
            for entry in entries:
                sums[entry] = sums[entry] + fold(jnp.where(bucket == entry, tile, 0.0))
        for entry in range(32):
            bias_out[0, entry * 8 : (entry + 1) * 8, :] = sums[entry]


def attend_back_call(info, att, grad, queries, keys, values):
    tall, span = keys.shape
    width = queries.shape[1] // 2
    heads = tall // HEAD_DIM
    return pl.pallas_call(
        attend_back_kernel,
        out_shape=(
            jax.ShapeDtypeStruct((tall, 2 * width), BF16),
            jax.ShapeDtypeStruct((tall, span), F32),
            jax.ShapeDtypeStruct((tall, span), F32),
            jax.ShapeDtypeStruct((heads, 256, LANES), F32),
        ),
        grid=(heads, 2),
        in_specs=[
            whole(pltpu.SMEM),
            pl.BlockSpec((1, span, width), lambda h, i: (h, 0, i)),
            pl.BlockSpec((HEAD_DIM, width), lambda h, i: (h, i)),
            pl.BlockSpec((HEAD_DIM, width), lambda h, i: (h, i)),
            pl.BlockSpec((HEAD_DIM, span), lambda h, i: (h, 0)),
            pl.BlockSpec((HEAD_DIM, span), lambda h, i: (h, 0)),
        ],
        out_specs=(
            pl.BlockSpec((HEAD_DIM, width), lambda h, i: (h, i)),
            pl.BlockSpec((HEAD_DIM, span), lambda h, i: (h, 0)),
            pl.BlockSpec((HEAD_DIM, span), lambda h, i: (h, 0)),
            pl.BlockSpec((1, 256, LANES), lambda h, i: (h, 0, 0)),
        ),
        scratch_shapes=[
            pltpu.VMEM((2 * span, LANES), F32),
            pltpu.VMEM((span, width), F32),
            pltpu.VMEM((span, width), BF16),
        ],
        compiler_params=params(24),
        cost_estimate=cost(heads * span * width * 2 * 2048, 8e6),
        name="attend_back",
    )(info, att, grad, queries, keys, values)


def project_kernel(info, blocks, ctx_own, ctx_other, wo_own, wo_core, wo_chip, wo_both, gain, hid, nrm):
    step = pl.program_id(0)
    core = info[1]
    rows = wo_own.shape[1]
    total = blocks[0].astype(F32)
    for slot in range(2):
        part = slice(slot * rows, (slot + 1) * rows)
        total = total + dot(pick(wo_own[...], wo_core[...], core, slot), ctx_own[part, :])
        total = total + dot(pick(wo_chip[...], wo_both[...], core, slot), ctx_other[part, :])
    scale = lax.rsqrt(jnp.mean(total * total, axis=0, keepdims=True) + EPSILON)
    nrm[...] = (total * scale * wide(gain[...], total.shape[1])).astype(BF16)

    @pl.when(step == 0)
    def _():
        hid[...] = total


def project_call(info, blocks, ctx_own, ctx_other, wos, gain):
    _, depth, width = blocks.shape
    tall = ctx_own.shape[0]
    return pl.pallas_call(
        project_kernel,
        out_shape=(
            jax.ShapeDtypeStruct((depth, width), F32),
            jax.ShapeDtypeStruct((depth, 2 * width), BF16),
        ),
        grid=(2,),
        in_specs=[
            whole(pltpu.SMEM),
            pl.BlockSpec((1, depth, width), lambda i: (i, 0, 0)),
            pl.BlockSpec((tall, width), lambda i: (0, i)),
            pl.BlockSpec((tall, width), lambda i: (0, 1 - i)),
            *[fixed(w.shape) for w in wos],
            fixed((depth, LANES)),
        ],
        out_specs=(
            pl.BlockSpec((depth, width), lambda i: (0, 0)),
            pl.BlockSpec((depth, width), lambda i: (0, i)),
        ),
        compiler_params=params(32),
        cost_estimate=cost(2 * depth * tall * width * 4, 8e6),
        name="project",
    )(info, blocks, ctx_own, ctx_other, *wos, gain)


def columns(total, chunk=256):
    return [(at, min(chunk, total - at)) for at in range(0, total, chunk)]


def hidden_kernel(first, second, w_ref, h_out, a_out, b_out):
    step = pl.program_id(0)
    rows = jnp.where(step < 2, first[...], second[...]).T
    for at, size in columns(w_ref.shape[2]):
        part = pl.ds(at, size)
        gate = dot(rows, w_ref[0, :, part])
        up = dot(rows, w_ref[1, :, part])
        square = gate * gate
        curve = jnp.tanh(GELU_SCALE * gate * (1.0 + GELU_CUBE * square))
        half = 0.5 * (1.0 + curve)
        value = gate * half
        slope = half + 0.5 * gate * (1.0 - curve * curve) * (
            GELU_SCALE * (1.0 + 3.0 * GELU_CUBE * square)
        )
        h_out[:, part] = (value * up).astype(BF16)
        a_out[:, part] = (up * slope).astype(BF16)
        b_out[:, part] = value.astype(BF16)


def hidden_call(first, second, weights):
    depth, both = first.shape
    width = both // 2
    hidden = weights.shape[2]
    out = jax.ShapeDtypeStruct((2 * both, hidden), BF16)
    spec = pl.BlockSpec((width, hidden), lambda i: (i, 0))
    return pl.pallas_call(
        hidden_kernel,
        out_shape=(out, out, out),
        grid=(4,),
        in_specs=[
            pl.BlockSpec((depth, width), lambda i: (0, jnp.minimum(i, 1))),
            pl.BlockSpec((depth, width), lambda i: (0, jnp.maximum(i - 2, 0))),
            fixed(weights.shape),
        ],
        out_specs=(spec, spec, spec),
        compiler_params=params(36),
        cost_estimate=cost(2 * depth * hidden * 2 * both * 2, 14e6, 2 * both * hidden),
        name="hidden",
    )(first, second, weights)


def slopes_kernel(first, second, wd_ref, w_ref, a_ref, b_ref, dg_out, dx_out):
    step = pl.program_id(0)
    rows = jnp.where(step < 2, first[...], second[...]).T
    for at, size in columns(wd_ref.shape[1]):
        part = pl.ds(at, size)
        grad = dot(rows, wd_ref[:, part])
        dg_out[0, :, part] = (grad * a_ref[:, part].astype(F32)).astype(BF16)
        dg_out[1, :, part] = (grad * b_ref[:, part].astype(F32)).astype(BF16)
    total = dot(w_ref[0], dg_out[0], NT) + dot(w_ref[1], dg_out[1], NT)
    dx_out[...] = total.astype(BF16)


def slopes_call(first, second, w_down, weights, a_part, b_part):
    depth, both = first.shape
    width = both // 2
    hidden = weights.shape[2]
    spec = pl.BlockSpec((width, hidden), lambda i: (i, 0))
    return pl.pallas_call(
        slopes_kernel,
        out_shape=(
            jax.ShapeDtypeStruct((2, 2 * both, hidden), BF16),
            jax.ShapeDtypeStruct((depth, 2 * both), BF16),
        ),
        grid=(4,),
        in_specs=[
            pl.BlockSpec((depth, width), lambda i: (0, jnp.minimum(i, 1))),
            pl.BlockSpec((depth, width), lambda i: (0, jnp.maximum(i - 2, 0))),
            fixed(w_down.shape),
            fixed(weights.shape),
            spec,
            spec,
        ],
        out_specs=(
            pl.BlockSpec((2, width, hidden), lambda i: (0, i, 0)),
            pl.BlockSpec((depth, width), lambda i: (0, i)),
        ),
        compiler_params=params(44),
        cost_estimate=cost(2 * depth * hidden * 2 * both * 3, 20e6),
        name="slopes",
    )(first, second, w_down, weights, a_part, b_part)


def down_kernel(wd_ref, h_ref, out):
    out[...] = dot(wd_ref[...], h_ref[...], NT).astype(BF16)


def down_call(w_down, hidden):
    depth = w_down.shape[0]
    rows, inner = hidden.shape
    width = rows // 4
    return pl.pallas_call(
        down_kernel,
        out_shape=jax.ShapeDtypeStruct((depth, rows), BF16),
        grid=(4,),
        in_specs=[fixed(w_down.shape), pl.BlockSpec((width, inner), lambda i: (i, 0))],
        out_specs=pl.BlockSpec((depth, width), lambda i: (0, i)),
        compiler_params=params(24),
        cost_estimate=cost(2 * depth * rows * inner, 8e6),
        name="down",
    )(w_down, hidden)


def outer_kernel(first, second, right, out):
    both = first.shape[1]
    total = dot(first[...], right[0, :both, :]) + dot(second[...], right[0, both:, :])
    out[0] = total.astype(BF16)


def outer_call(first, second, right):
    depth, both = first.shape
    count, rows, inner = right.shape
    tile = depth // 4
    return pl.pallas_call(
        outer_kernel,
        out_shape=jax.ShapeDtypeStruct((count, depth, inner), BF16),
        grid=(count, 4),
        in_specs=[
            pl.BlockSpec((tile, both), lambda n, i: (i, 0)),
            pl.BlockSpec((tile, both), lambda n, i: (i, 0)),
            pl.BlockSpec((1, rows, inner), lambda n, i: (n, 0, 0)),
        ],
        out_specs=pl.BlockSpec((1, tile, inner), lambda n, i: (n, i, 0)),
        compiler_params=params(32),
        cost_estimate=cost(2 * depth * rows * inner * count, count * 9e6),
        name="outer",
    )(first, second, right)


def middle_kernel(
    info, mine, theirs, hid, gain, cot, wo_own, wo_core, wo_chip, wo_both, gh_out, ga_out, go_out, gx_out
):
    core, length, base = info[1], info[2], info[3]
    incoming = mine[...].astype(F32) + theirs[...].astype(F32)
    hidden = hid[...]
    width = hidden.shape[1]
    scale = lax.rsqrt(jnp.mean(hidden * hidden, axis=0, keepdims=True) + EPSILON)
    unit = hidden * scale
    grad = incoming * wide(gain[...], width)
    slope = grad - unit * jnp.mean(grad * unit, axis=0, keepdims=True)
    position = base + lax.broadcasted_iota(jnp.int32, (1, width), 1)
    out = jnp.where(position < length, cot[...].astype(F32), 0.0) + scale * slope
    gh_out[...] = out
    grad_attn = out.astype(BF16)
    ga_out[...] = grad_attn
    rows = wo_own.shape[1]
    for slot in range(2):
        part = slice(slot * rows, (slot + 1) * rows)
        go_out[part, :] = dot(pick(wo_own[...], wo_core[...], core, slot), grad_attn, TN).astype(BF16)
        gx_out[part, :] = dot(pick(wo_chip[...], wo_both[...], core, slot), grad_attn, TN).astype(BF16)


def middle_call(info, mine, theirs, hid, gain, cot, wos):
    depth, width = hid.shape
    tall = 2 * wos[0].shape[1]
    wide_shape = jax.ShapeDtypeStruct((depth, width), F32)
    return pl.pallas_call(
        middle_kernel,
        out_shape=(
            wide_shape,
            jax.ShapeDtypeStruct((depth, width), BF16),
            jax.ShapeDtypeStruct((tall, width), BF16),
            jax.ShapeDtypeStruct((tall, width), BF16),
        ),
        in_specs=[whole(pltpu.SMEM)] + [whole(pltpu.VMEM)] * 9,
        out_specs=(whole(pltpu.VMEM),) * 4,
        compiler_params=params(32),
        cost_estimate=cost(2 * depth * tall * width * 2, 10e6),
        name="middle",
    )(info, mine, theirs, hid, gain, cot, *wos)


def gains_kernel(info, mine, theirs, hid, grad_attn, ctx_own, ctx_other, gain_out, dwo_out):
    incoming = mine[...].astype(F32) + theirs[...].astype(F32)
    hidden = hid[...]
    scale = lax.rsqrt(jnp.mean(hidden * hidden, axis=0, keepdims=True) + EPSILON)
    gain_out[...] = jnp.sum(incoming * (hidden * scale), axis=1, keepdims=True)
    rows = dwo_out.shape[2]
    for slot in range(2):
        part = slice(slot * rows, (slot + 1) * rows)
        dwo_out[slot] = dot(grad_attn[...], ctx_own[part, :], NT).astype(BF16)
        dwo_out[2 + slot] = dot(grad_attn[...], ctx_other[part, :], NT).astype(BF16)


def gains_call(info, mine, theirs, hid, grad_attn, ctx_own, ctx_other):
    depth, width = hid.shape
    rows = ctx_own.shape[0] // 2
    return pl.pallas_call(
        gains_kernel,
        out_shape=(
            jax.ShapeDtypeStruct((depth, 1), F32),
            jax.ShapeDtypeStruct((4, depth, rows), BF16),
        ),
        in_specs=[whole(pltpu.SMEM)] + [whole(pltpu.VMEM)] * 6,
        out_specs=(whole(pltpu.VMEM),) * 2,
        compiler_params=params(32),
        cost_estimate=cost(2 * depth * rows * width * 4, 6e6),
        name="gains",
    )(info, mine, theirs, hid, grad_attn, ctx_own, ctx_other)


def weights_kernel(normed, grads, out):
    rows = out.shape[2]
    width = normed.shape[2]
    for part in range(3):
        total = dot(normed[0], grads[part, :, :width], NT)
        for block in range(1, normed.shape[0]):
            at = slice(block * width, (block + 1) * width)
            total = total + dot(normed[block], grads[part, :, at], NT)
        out[part] = total.astype(BF16)


def weights_call(normed, grads):
    count, depth, width = normed.shape
    rows = grads.shape[1]
    tile = depth // 2
    return pl.pallas_call(
        weights_kernel,
        out_shape=jax.ShapeDtypeStruct((3, depth, rows), BF16),
        grid=(2,),
        in_specs=[pl.BlockSpec((count, tile, width), lambda i: (0, i, 0)), fixed(grads.shape)],
        out_specs=pl.BlockSpec((3, tile, rows), lambda i: (0, i, 0)),
        compiler_params=params(32),
        cost_estimate=cost(2 * depth * rows * 3 * width * count, 6e6),
        name="weights",
    )(normed, grads)


def entry_kernel(info, d_own, d_other, w_own, w_core, w_chip, w_both, x_ref, gain, gh_ref, out, gain_out):
    core = info[1]
    rows = w_own.shape[2]
    total = None
    for part in range(3):
        for slot in range(2):
            at = slice(slot * rows, (slot + 1) * rows)
            one = dot(pick(w_own[part], w_core[part], core, slot), d_own[part, at, :])
            two = dot(pick(w_chip[part], w_both[part], core, slot), d_other[part, at, :])
            total = one + two if total is None else total + one + two
    values = x_ref[...].astype(F32)
    scale = lax.rsqrt(jnp.mean(values * values, axis=0, keepdims=True) + EPSILON)
    unit = values * scale
    gain_out[...] = jnp.sum(total * unit, axis=1, keepdims=True)
    grad = total * wide(gain[...], total.shape[1])
    slope = grad - unit * jnp.mean(grad * unit, axis=0, keepdims=True)
    out[...] = gh_ref[...] + scale * slope


def entry_call(info, d_own, d_other, ws, x_own, gain, grad_hidden):
    depth, width = grad_hidden.shape
    rows = d_own.shape[1]
    return pl.pallas_call(
        entry_kernel,
        out_shape=(
            jax.ShapeDtypeStruct((depth, width), F32),
            jax.ShapeDtypeStruct((depth, 1), F32),
        ),
        in_specs=[whole(pltpu.SMEM)] + [whole(pltpu.VMEM)] * 9,
        out_specs=(whole(pltpu.VMEM),) * 2,
        compiler_params=params(32),
        cost_estimate=cost(2 * depth * rows * 6 * width, 12e6),
        name="entry",
    )(info, d_own, d_other, *ws, x_own, gain, grad_hidden)


def ring_rows(count):
    if count % 2 or count < 4:
        return list(range(count))
    return list(range(0, count, 2)) + list(range(count - 1, 0, -2))


def device_pairs(row_total, col_total, move):
    pairs = []
    for row in range(row_total):
        for col in range(col_total):
            other_row, other_col = move(row, col)
            pairs.append((row * col_total + col, other_row * col_total + other_col))
    return pairs


class Moves:
    def __init__(self, row_total, col_total):
        order = ring_rows(row_total)
        place = {row: at for at, row in enumerate(order)}
        step = lambda by: device_pairs(
            row_total, col_total, lambda r, c: (order[(place[r] + by) % row_total], c)
        )
        self.count = row_total
        self.order = order
        self.place = [place[row] for row in range(row_total)]
        self.right_pairs, self.left_pairs = step(1), step(-1)
        self.chip_pairs = device_pairs(row_total, col_total, lambda r, c: (r, (c + 2) % 4))
        self.core_pairs = device_pairs(row_total, col_total, lambda r, c: (r, c ^ 1))
        row = lax.axis_index("row")
        spot = jnp.array(self.place, jnp.int32)[row]
        around = (spot + jnp.arange(row_total, dtype=jnp.int32)) % row_total
        self.rows = jnp.array(order, jnp.int32)[around]

    def send(self, array, pairs):
        return lax.ppermute(array, ("row", "col"), pairs)

    def right(self, array):
        return self.send(array, self.right_pairs)

    def left(self, array):
        return self.send(array, self.left_pairs)

    def chip(self, array):
        return self.send(array, self.chip_pairs)

    def core(self, array):
        return self.send(array, self.core_pairs)

    def row_at(self, distance):
        return self.rows[distance % self.count]

    def gather(self, shard):
        parts, rows, cols = shard.shape
        out = jnp.zeros((parts, self.count * rows, cols), shard.dtype)

        def place(out, piece, distance, begin=0):
            at = self.row_at(distance) * rows + begin
            return lax.dynamic_update_slice(out, piece, (0, at, 0))

        out = place(out, shard, 0)
        right = left = shard
        for hop in range(1, (self.count - 1) // 2 + 1):
            right, left = self.right(right), self.left(left)
            out = place(place(out, right, -hop), left, hop)
        if self.count % 2 == 0:
            far = self.count // 2
            cut = (rows // 2 + 7) // 8 * 8
            first, last = self.right(right[:, :cut]), self.left(left[:, cut:])
            out = place(place(out, first, -far), last, far, cut)
        return out

    def reduce(self, full):
        parts, total, cols = full.shape
        rows = total // self.count

        def part(distance, begin=0, end=rows):
            at = self.row_at(distance) * rows + begin
            return lax.dynamic_slice(full, (0, at, 0), (parts, end - begin, cols))

        add = lambda one, two: (one.astype(F32) + two.astype(F32)).astype(BF16)
        half = (self.count - 1) // 2
        far = self.count // 2
        cut = (rows // 2 + 7) // 8 * 8
        right = self.right(part(far, 0, cut))
        left = self.left(part(-far, cut, rows))
        right = jnp.concatenate([add(part(half, 0, cut), right), part(half, cut, rows)], axis=1)
        left = jnp.concatenate([part(-half, 0, cut), add(part(-half, cut, rows), left)], axis=1)
        for hop in range(half - 1, 0, -1):
            right, left = self.right(right), self.left(left)
            right, left = add(part(hop), right), add(part(-hop), left)
        right, left = self.right(right), self.left(left)
        return part(0).astype(F32) + right.astype(F32) + left.astype(F32)

    def total(self, array):
        array = array + self.core(array)
        array = array + self.chip(array)
        bit = 1
        while bit < self.count:
            pairs = device_pairs(self.count, 4, lambda r, c: (r ^ bit, c))
            array = array + self.send(array, pairs)
            bit *= 2
        return array


def paired_body(
    tokens,
    lengths,
    out_grad,
    gain_attn,
    w_query,
    w_key,
    w_value,
    w_attn_out,
    bias_table,
    gain_ff,
    w_gate,
    w_up,
    w_down,
):
    width, depth = tokens.shape
    rows = w_query.shape[1]
    tall = 2 * rows
    moves = Moves(lax.axis_size("row"), lax.axis_size("col"))
    col = lax.axis_index("col").astype(jnp.int32)
    chip, core = col // 2, col % 2
    base = lambda x, c: (2 * x + c) * width
    info = jnp.stack(
        [
            chip,
            core,
            lengths[0],
            base(chip, core),
            base(1 - chip, core),
            base(chip, 1 - core),
            base(1 - chip, 1 - core),
            jnp.zeros((), jnp.int32),
        ]
    ).astype(jnp.int32)
    lanes = lambda gain: jnp.broadcast_to(gain[:, None], (depth, LANES))
    gain_one, gain_two = lanes(gain_attn), lanes(gain_ff)

    x_own = tokens.T
    x_chip = moves.chip(x_own)
    attn_shard = jnp.stack([w_query, w_key, w_value, w_attn_out.T])
    attn_own = moves.gather(attn_shard)
    ff_weights = moves.gather(jnp.stack([w_gate, w_up]))
    w_down_full = moves.gather(w_down.T[None])[0]
    x_pair = jnp.stack([x_own, x_chip])
    blocks = jnp.concatenate([x_pair, moves.core(x_pair)], axis=0)
    attn_core = moves.core(attn_own)

    position = base(chip, core) + jnp.arange(width, dtype=jnp.int32)
    row_mask = (position < lengths[0])[None, :]
    cot_own = out_grad.T
    cot_masked = jnp.where(row_mask, cot_own, jnp.zeros((), BF16))

    normed, q_t, k_t, v_t = qkv_call(info, blocks, gain_one, attn_own[:3], attn_core[:3])
    att, ctx_own = attend_call(info, bias_table, q_t, k_t, v_t)
    ctx_other = moves.chip(ctx_own)
    attn_chip = moves.chip(attn_own)
    attn_both = moves.core(attn_chip)
    wos = (attn_own[3], attn_core[3], attn_chip[3], attn_both[3])
    hid, ff_first = project_call(info, x_pair, ctx_own, ctx_other, wos, gain_two)
    ff_second = moves.core(ff_first)

    cot_chip = moves.chip(cot_masked)
    cot_first = jnp.concatenate([cot_masked, cot_chip], axis=1)
    cot_second = moves.core(cot_first)

    hidden, a_part, b_part = hidden_call(ff_first, ff_second, ff_weights)
    grad_down_part = outer_call(cot_first, cot_second, hidden[None])
    grad_pair, dx = slopes_call(cot_first, cot_second, w_down_full, ff_weights, a_part, b_part)
    dx_sum = dx[:, : 2 * width].astype(F32) + moves.core(dx[:, 2 * width :]).astype(F32)
    dx_sum = dx_sum.astype(BF16)
    dx_mine, dx_theirs = dx_sum[:, :width], moves.chip(dx_sum[:, width:])
    grad_ff_part = outer_call(ff_first, ff_second, grad_pair)
    branch = down_call(w_down_full, hidden)
    branch = (branch[:, : 2 * width].astype(F32) + moves.core(branch[:, 2 * width :]).astype(F32)).astype(BF16)
    branch_theirs = moves.chip(branch[:, width:])
    branch_sum = branch[:, :width].astype(F32) + branch_theirs.astype(F32)
    output = jnp.where(row_mask, hid + branch_sum, 0.0).astype(BF16).T

    grad_down = moves.reduce(grad_down_part)
    grad_gate_up = moves.reduce(grad_ff_part)

    grad_hidden, grad_attn, g_own, g_send = middle_call(
        info, dx_mine, dx_theirs, hid, gain_two, cot_own, wos
    )
    g_ctx = jnp.concatenate([g_own, moves.chip(g_send)], axis=1)
    gain_ff_part, dwo = gains_call(
        info, dx_mine, dx_theirs, hid, grad_attn, ctx_own[:, :width], ctx_other[:, width:]
    )
    dwo = dwo.reshape(2, 2, depth, rows)
    mine = lax.dynamic_index_in_dim(dwo, core, 1, keepdims=False)
    rest = lax.dynamic_index_in_dim(dwo, 1 - core, 1, keepdims=False)
    dwo = (mine.astype(F32) + moves.core(rest).astype(F32)).astype(BF16)
    dwo = (dwo[0].astype(F32) + moves.chip(dwo[1]).astype(F32)).astype(BF16)

    dq, dk, dv, bias_sums = attend_back_call(info, att, g_ctx, q_t, k_t, v_t)
    dkv = jnp.stack([dk, dv])
    turned = moves.core(dkv)
    turned = jnp.concatenate([turned[:, :, 2 * width :], turned[:, :, : 2 * width]], axis=2)
    dkv = (dkv + turned).astype(BF16)
    dq_core = moves.core(dq)
    d_pair = jnp.stack([dq, dkv[0, :, : 2 * width], dkv[1, :, : 2 * width]])
    d_chip = moves.chip(d_pair[:, :, width:])
    d_mine = lax.dynamic_slice_in_dim(
        jnp.concatenate([jnp.concatenate([dq, dq_core], axis=1)[None], dkv], axis=0), core * rows, rows, 1
    )
    grad_attn_part = jnp.concatenate([weights_call(normed, d_mine), dwo[None]], axis=0)
    grad_attn_all = moves.reduce(grad_attn_part)
    ws = (attn_own[:3], attn_core[:3], attn_chip[:3], attn_both[:3])
    input_grad, gain_attn_part = entry_call(
        info, d_pair[:, :, :width], d_chip, ws, x_own, gain_one, grad_hidden
    )

    heads = tall // HEAD_DIM
    bias_part = jnp.sum(bias_sums.reshape(heads, 32, 8, LANES), axis=(2, 3)).T
    bias_part = lax.dynamic_update_slice(jnp.zeros((32, HEADS), F32), bias_part, (0, chip * heads))
    small = jnp.concatenate([gain_attn_part[:, 0], gain_ff_part[:, 0], bias_part.reshape(-1)])
    pad = -small.shape[0] % 1024
    small = moves.total(jnp.pad(small, (0, pad)).reshape(-1, LANES)).reshape(-1)
    return (
        output,
        input_grad.T,
        small[:depth],
        grad_attn_all[0],
        grad_attn_all[1],
        grad_attn_all[2],
        grad_attn_all[3].T,
        small[2 * depth : 2 * depth + 32 * HEADS].reshape(32, HEADS),
        small[depth : 2 * depth],
        grad_gate_up[0],
        grad_gate_up[1],
        grad_down[0].T,
    )


def bucket_index(offsets):
    magnitude = jnp.abs(offsets)
    far_bucket = 8 + sum(((magnitude >= limit).astype(jnp.int32) for limit in FAR_STEPS))
    near_bucket = jnp.where(magnitude < 8, magnitude, far_bucket)
    return near_bucket + jnp.where(offsets > 0, 16, 0)


def root_scale(values, gain):
    return values * lax.rsqrt(jnp.mean(values * values, axis=-1, keepdims=True) + EPSILON) * gain


def gated_product(gate_part, up_part):
    return jax.nn.gelu(gate_part, approximate=True) * up_part


def matmul(left, right):
    return jnp.dot(left, right, preferred_element_type=jnp.float32)


def spread_rows(line, row_total, column_total):
    line_width = line.shape[0]
    tiled_line = jnp.tile(line, row_total + 1)[: row_total * (line_width + 1)]
    shifted = tiled_line.reshape(row_total, line_width + 1)
    return shifted[::-1, :column_total]


def fold_rows(matrix):
    row_total, column_total = matrix.shape
    padded = jnp.pad(matrix[::-1], ((0, 0), (0, row_total)))
    flattened = padded.reshape(-1)[: row_total * (column_total + row_total - 1)]
    return jnp.sum(flattened.reshape(row_total, column_total + row_total - 1), axis=0)


def body(
    tokens,
    lengths,
    out_grad,
    gain_attn,
    w_query,
    w_key,
    w_value,
    w_attn_out,
    bias_table,
    gain_ff,
    w_gate,
    w_up,
    w_down,
):
    tok_rows = tokens.shape[0]
    seq_len = tok_rows * lax.axis_size("col")
    first_row = lax.axis_index("col") * tok_rows
    doc_length = lengths[0]
    local_pos = first_row + jnp.arange(tok_rows, dtype=jnp.int32)
    row_mask = (local_pos < doc_length).astype(jnp.float32)[:, None]
    key_valid = jnp.arange(seq_len, dtype=jnp.int32) < doc_length
    row_query, row_key, row_value, row_out, full_gate, full_up, full_down = (
        lax.all_gather(w_query, "row", axis=0, tiled=True),
        lax.all_gather(w_key, "row", axis=0, tiled=True),
        lax.all_gather(w_value, "row", axis=0, tiled=True),
        lax.all_gather(w_attn_out, "row", axis=1, tiled=True),
        lax.all_gather(w_gate, "row", axis=0, tiled=True),
        lax.all_gather(w_up, "row", axis=0, tiled=True),
        lax.all_gather(w_down, "row", axis=1, tiled=True),
    )
    full_query, full_key, full_value, full_out = (
        lax.all_gather(row_query, "col", axis=1, tiled=True),
        lax.all_gather(row_key, "col", axis=1, tiled=True),
        lax.all_gather(row_value, "col", axis=1, tiled=True),
        lax.all_gather(row_out, "col", axis=0, tiled=True),
    )
    inputs_float = tokens.astype(jnp.float32)
    normed = root_scale(inputs_float, gain_attn).astype(jnp.bfloat16)
    queries = matmul(normed, full_query).astype(jnp.bfloat16)
    own_keys = matmul(normed, full_key).astype(jnp.bfloat16)
    own_values = matmul(normed, full_value).astype(jnp.bfloat16)
    keys_all, values_all = (
        lax.all_gather(own_keys, "col", axis=0, tiled=True),
        lax.all_gather(own_values, "col", axis=0, tiled=True),
    )
    offset_span = seq_len + tok_rows - 1
    offsets = jnp.arange(offset_span, dtype=jnp.int32) - (tok_rows - 1) - first_row
    onehot = (
        bucket_index(offsets)[:, None] == jnp.arange(bias_table.shape[0], dtype=jnp.int32)[None, :]
    ).astype(jnp.float32)
    bias_lines = jnp.dot(
        onehot, bias_table, precision=PRECISION_MAX, preferred_element_type=jnp.float32
    ).T

    def head_scores(head_index):
        head_start = head_index * HEAD_DIM
        query_head = queries[:, head_start : head_start + HEAD_DIM]
        key_head = keys_all[:, head_start : head_start + HEAD_DIM]
        scores = jnp.einsum("qd,kd->qk", query_head, key_head, preferred_element_type=jnp.float32)
        scores = scores + spread_rows(bias_lines[head_index], tok_rows, seq_len)
        return jnp.where(key_valid[None, :], scores, -1e30)

    contexts = []
    log_totals = []
    for head_index in range(HEADS):
        masked = head_scores(head_index)
        row_peak = jnp.max(masked, axis=1, keepdims=True)
        log_total = row_peak + jnp.log(jnp.sum(jnp.exp(masked - row_peak), axis=1, keepdims=True))
        attention = jnp.exp(masked - log_total)
        value_head = values_all[:, head_index * HEAD_DIM : (head_index + 1) * HEAD_DIM]
        contexts.append(
            jnp.einsum(
                "qk,kd->qd",
                attention.astype(jnp.bfloat16),
                value_head,
                preferred_element_type=jnp.float32,
            )
        )
        log_totals.append(log_total)
    context = jnp.concatenate(contexts, axis=1).astype(jnp.bfloat16)
    hidden = inputs_float + matmul(context, full_out)
    normed_ff = root_scale(hidden, gain_ff).astype(jnp.bfloat16)
    grad_out = out_grad.astype(jnp.float32) * row_mask
    ff_rows = lax.all_gather(normed_ff, "col", axis=0, tiled=True)
    hidden_ff = gated_product(matmul(ff_rows, full_gate), matmul(ff_rows, full_up)).astype(
        jnp.bfloat16
    )
    ff_branch = lax.psum_scatter(
        matmul(hidden_ff, full_down).astype(jnp.bfloat16), "col", scatter_dimension=0, tiled=True
    ).astype(jnp.float32)
    output = (row_mask * (hidden + ff_branch)).astype(jnp.bfloat16)
    cot_rows = lax.all_gather(grad_out.astype(jnp.bfloat16), "col", axis=0, tiled=True)
    gate_proj = matmul(ff_rows, full_gate)
    up_proj = matmul(ff_rows, full_up)
    product_value, gelu_pull = jax.vjp(gated_product, gate_proj, up_proj)
    hidden_back = product_value.astype(jnp.bfloat16)
    grad_down_part = jnp.einsum(
        "rf,rd->fd", hidden_back, cot_rows, preferred_element_type=jnp.float32
    )
    grad_hidden_ff = jnp.einsum(
        "rd,fd->rf", cot_rows, full_down, preferred_element_type=jnp.float32
    )
    grad_gate_float, grad_up_float = gelu_pull(grad_hidden_ff)
    grad_gate_proj = grad_gate_float.astype(jnp.bfloat16)
    grad_up_proj = grad_up_float.astype(jnp.bfloat16)
    grad_gate_part = jnp.einsum(
        "rd,rf->df", ff_rows, grad_gate_proj, preferred_element_type=jnp.float32
    )
    grad_up_part = jnp.einsum(
        "rd,rf->df", ff_rows, grad_up_proj, preferred_element_type=jnp.float32
    )
    grad_normed_ff = lax.psum_scatter(
        (
            jnp.einsum("rf,df->rd", grad_gate_proj, full_gate, preferred_element_type=jnp.float32)
            + jnp.einsum("rf,df->rd", grad_up_proj, full_up, preferred_element_type=jnp.float32)
        ).astype(jnp.bfloat16),
        "col",
        scatter_dimension=0,
        tiled=True,
    ).astype(jnp.float32)
    norm_value, norm_pull = jax.vjp(root_scale, hidden, gain_ff)
    grad_hidden_norm, grad_gain_ff_part = norm_pull(grad_normed_ff)
    grad_hidden = grad_out + grad_hidden_norm
    grad_attn = grad_hidden.astype(jnp.bfloat16)
    grad_out_part = jnp.einsum("ti,td->id", context, grad_attn, preferred_element_type=jnp.float32)
    grad_context = jnp.einsum(
        "td,id->ti", grad_attn, full_out, preferred_element_type=jnp.float32
    ).astype(jnp.bfloat16)
    grad_query_heads = []
    grad_key_heads = []
    grad_value_heads = []
    diagonal_lines = []
    for head_index in range(HEADS):
        head_start = head_index * HEAD_DIM
        query_head = queries[:, head_start : head_start + HEAD_DIM]
        key_head = keys_all[:, head_start : head_start + HEAD_DIM]
        value_head = values_all[:, head_start : head_start + HEAD_DIM]
        grad_ctx_head = grad_context[:, head_start : head_start + HEAD_DIM]
        attention = jnp.exp(head_scores(head_index) - log_totals[head_index])
        grad_attention = jnp.einsum(
            "qd,kd->qk", grad_ctx_head, value_head, preferred_element_type=jnp.float32
        )
        row_inner = jnp.sum(attention * grad_attention, axis=1, keepdims=True)
        grad_scores = (attention * (grad_attention - row_inner)).astype(jnp.bfloat16)
        grad_query_heads.append(
            jnp.einsum("qk,kd->qd", grad_scores, key_head, preferred_element_type=jnp.float32)
        )
        grad_key_heads.append(
            jnp.einsum("qk,qd->kd", grad_scores, query_head, preferred_element_type=jnp.float32)
        )
        grad_value_heads.append(
            jnp.einsum(
                "qk,qd->kd",
                attention.astype(jnp.bfloat16),
                grad_ctx_head,
                preferred_element_type=jnp.float32,
            )
        )
        diagonal_lines.append(fold_rows(grad_scores.astype(jnp.float32)))
    grad_bias_part = jnp.einsum(
        "eb,he->bh",
        onehot,
        jnp.stack(diagonal_lines, axis=0),
        precision=PRECISION_MAX,
        preferred_element_type=jnp.float32,
    )
    grad_queries = jnp.concatenate(grad_query_heads, axis=1).astype(jnp.bfloat16)
    key_partial = jnp.concatenate(grad_key_heads, axis=1)
    value_partial = jnp.concatenate(grad_value_heads, axis=1)
    key_summed, value_summed = (
        lax.psum_scatter(
            key_partial.astype(jnp.bfloat16), "col", scatter_dimension=0, tiled=True
        ).astype(jnp.float32),
        lax.psum_scatter(
            value_partial.astype(jnp.bfloat16), "col", scatter_dimension=0, tiled=True
        ).astype(jnp.float32),
    )
    grad_keys = key_summed.astype(jnp.bfloat16)
    grad_values = value_summed.astype(jnp.bfloat16)
    grad_query_part = jnp.einsum(
        "td,ti->di", normed, grad_queries, preferred_element_type=jnp.float32
    )
    grad_key_part = jnp.einsum("td,ti->di", normed, grad_keys, preferred_element_type=jnp.float32)
    grad_value_part = jnp.einsum(
        "td,ti->di", normed, grad_values, preferred_element_type=jnp.float32
    )
    grad_normed = (
        jnp.einsum("ti,di->td", grad_queries, full_query, preferred_element_type=jnp.float32)
        + jnp.einsum("ti,di->td", grad_keys, full_key, preferred_element_type=jnp.float32)
        + jnp.einsum("ti,di->td", grad_values, full_value, preferred_element_type=jnp.float32)
    )
    first_value, first_pull = jax.vjp(root_scale, inputs_float, gain_attn)
    grad_input_norm, grad_gain_attn_part = first_pull(grad_normed)
    input_grad = grad_hidden + grad_input_norm
    cols_query, cols_key, cols_value, cols_out = (
        lax.psum_scatter(
            grad_query_part.astype(jnp.bfloat16), "col", scatter_dimension=1, tiled=True
        ).astype(jnp.float32),
        lax.psum_scatter(
            grad_key_part.astype(jnp.bfloat16), "col", scatter_dimension=1, tiled=True
        ).astype(jnp.float32),
        lax.psum_scatter(
            grad_value_part.astype(jnp.bfloat16), "col", scatter_dimension=1, tiled=True
        ).astype(jnp.float32),
        lax.psum_scatter(
            grad_out_part.astype(jnp.bfloat16), "col", scatter_dimension=0, tiled=True
        ).astype(jnp.float32),
    )
    grad_query, grad_key, grad_value, grad_attn_out, grad_gate, grad_up, grad_down = (
        lax.psum_scatter(
            cols_query.astype(jnp.bfloat16), "row", scatter_dimension=0, tiled=True
        ).astype(jnp.float32),
        lax.psum_scatter(
            cols_key.astype(jnp.bfloat16), "row", scatter_dimension=0, tiled=True
        ).astype(jnp.float32),
        lax.psum_scatter(
            cols_value.astype(jnp.bfloat16), "row", scatter_dimension=0, tiled=True
        ).astype(jnp.float32),
        lax.psum_scatter(
            cols_out.astype(jnp.bfloat16), "row", scatter_dimension=1, tiled=True
        ).astype(jnp.float32),
        lax.psum_scatter(
            grad_gate_part.astype(jnp.bfloat16), "row", scatter_dimension=0, tiled=True
        ).astype(jnp.float32),
        lax.psum_scatter(
            grad_up_part.astype(jnp.bfloat16), "row", scatter_dimension=0, tiled=True
        ).astype(jnp.float32),
        lax.psum_scatter(
            grad_down_part.astype(jnp.bfloat16), "row", scatter_dimension=1, tiled=True
        ).astype(jnp.float32),
    )
    grad_gain_attn, grad_bias, grad_gain_ff = lax.psum(
        (grad_gain_attn_part, grad_bias_part, grad_gain_ff_part), ("row", "col")
    )
    return (
        output,
        input_grad,
        grad_gain_attn,
        grad_query,
        grad_key,
        grad_value,
        grad_attn_out,
        grad_bias,
        grad_gain_ff,
        grad_gate,
        grad_up,
        grad_down,
    )


def paired(mesh):
    return mesh.shape["col"] == 4 and HEADS % 2 == 0 and mesh.shape["row"] == 8


def solution(mesh):
    placed = (
        P(("row", "col"), None),
        P("row"),
        P(("row", "col"), None),
        P(),
        P("row", "col"),
        P("row", "col"),
        P("row", "col"),
        P("col", "row"),
        P(),
        P(),
        P("row", "col"),
        P("row", "col"),
        P("col", "row"),
    )
    return jax.shard_map(
        paired_body if paired(mesh) else body,
        mesh=mesh,
        in_specs=placed,
        out_specs=(
            P(("row", "col"), None),
            P(("row", "col"), None),
            P(),
            P("row", "col"),
            P("row", "col"),
            P("row", "col"),
            P("col", "row"),
            P(),
            P(),
            P("row", "col"),
            P("row", "col"),
            P("col", "row"),
        ),
        check_vma=False,
    )
```
